128 devices in a mesh: energy: 32 (over z, y, x_lo), slab: 4 (over x_hi, core).
Axes of the slice: x: 4 (x_hi: 2, x_lo: 2; x = x_hi * 2 + x_lo), y: 4, z: 4, core: 2. Of those that a mesh axis runs over, the one named last changes fastest.
Arguments:
- energy_real: float32 [128], P('energy'), may hold values from -2 to 2
- energy_imag: float32 [128], P('energy'), may hold values from 1 to 2
- potential: float32 [4, 256], P('slab'), may hold values from -1.5 to 1.5
- onsite: float32 [4, 2, 256, 256], P('slab'), may hold values from -0.078125 to 0.078125
- coupling: float32 [4, 2, 256, 256], P('slab'), may hold values from -1.1 to 1.1
- deform: float32 [4, 256, 256], P('slab'), may hold values from 0.2 to 1
- offsets: int32 [8], replicated, may hold values from -8 to 8, as said below
- weights: int32 [8], replicated, may hold values from 8 to 40
Outputs:
- green: float32 [128, 4, 2, 256, 256], P('energy', 'slab')
- self_energy: float32 [128, 4, 2, 256, 256], P('energy', 'slab')
The draws below stay inside these ranges and needn't reach their ends.
Inputs may be any that keep to these rules, and one draw needn't show every extreme that they name: Eight offsets; -8 and 8 are always among them.
All inputs are finite; a program needn't handle non-finite values.
Results may differ from the reference program's by a relative error of at most 0.0001.
Values sent between devices are 32-bit elements; how exact they have to be, the bound alone decides.
No kernel may reach another device: no remote copies, remote signals or barrier semaphores. Data moves between devices by JAX's collectives and lax.ppermute only.
A program may use at most 128 MiB of HBM per device.

```python
import math
import jax
import jax.numpy as jnp
from jax import lax

M = 256
E_DEV = 4
OFFSETS = 8
SWEEPS = 3
OUTER = 2
NEWTON = 2
ENERGIES = 128
SLABS = 4


def draw_offsets(key, part):
    values = jax.random.randint(key, (OFFSETS,), -2 * E_DEV, 2 * E_DEV + 1)
    position = jnp.arange(OFFSETS)
    values = jnp.where(position == 0, -2 * E_DEV, jnp.where(position == 1, 2 * E_DEV, values))
    order = jax.random.permutation(jax.random.fold_in(key, 7), OFFSETS)
    return values[order].astype(jnp.int32)


def draw_coupling(key, part):
    key_size = jax.random.fold_in(key, 11)
    key_angle = jax.random.fold_in(key, 12)
    key_jitter = jax.random.fold_in(key, 13)
    shape = (SLABS, 2, M, M)
    magnitude = jnp.exp(jax.random.uniform(key_size, (SLABS, M), jnp.float32, math.log(0.5), math.log(0.95)))
    jitter = jnp.clip(jax.random.normal(key_jitter, shape, jnp.float32), -4.0, 4.0)
    angles = jax.random.uniform(key_angle, (SLABS, M), jnp.float32, -math.pi, math.pi)
    spread = 0.25 / math.sqrt(2.0 * M)
    identity = jnp.eye(M, dtype=jnp.float32)
    diagonal_real = (magnitude * jnp.cos(angles))[:, :, None] * identity
    diagonal_imag = (magnitude * jnp.sin(angles))[:, :, None] * identity
    return (jnp.stack([diagonal_real, diagonal_imag], axis=1) + spread * jitter).astype(jnp.float32)


def set_ends(values, rng, low, largest):
    extent = values.shape
    index_at = [jax.random.randint(jax.random.fold_in(rng, axis), (), 0, extent[axis]) for axis in range(len(extent))]
    values = values.at[tuple(index_at)].set(low)
    longest = extent.index(max(extent))
    index_at[longest] = (index_at[longest] + 1) % extent[longest]
    return values.at[tuple(index_at)].set(largest)


def steps_of(own_key, shape, shards, smallest, largest):
    level, own = 1.0, jax.random.fold_in(own_key, 6)
    for dim, shards_of in shards:
        heights = jnp.exp(jax.random.uniform(jax.random.fold_in(own, dim), (shards_of,), jnp.float32, smallest / len(shards), largest / len(shards)))
        level = level * jnp.repeat(heights, shape[dim] // shards_of).reshape([-1 if axis == dim else 1 for axis in range(len(shape))])
    return level


def gaussian(stream_key, shape, deviation, reach, split=(), kind=jnp.bfloat16):
    gain = steps_of(stream_key, shape, split, -0.22, 0.18) if split else 1.0
    entries = jax.random.normal(stream_key, shape, jnp.float32) * deviation * gain
    return jnp.minimum(jnp.maximum(entries, -reach), reach).astype(kind)


def setup_inputs(seed: int = 0) -> dict:
    arg_keys = jax.random.split(jax.random.key(seed), 9)
    energy_real = jnp.clip(jax.random.uniform(arg_keys[0], (ENERGIES,), jnp.float32, -2.0, 2.0) * steps_of(arg_keys[0], (ENERGIES,), ((0, 32),), -0.4, 0.0), -2.0, 2.0)
    energy_imag = jnp.clip(jnp.exp(math.log(2.0) - 0.6931472 * jax.random.uniform(arg_keys[1], (ENERGIES,), jnp.float32) ** steps_of(arg_keys[1], (ENERGIES,), ((0, 32),), -0.2, 0.2)), 1.0, 2.0)
    potential = jnp.clip(jax.random.uniform(arg_keys[2], (SLABS, M), jnp.float32, -1.5, 1.5) * steps_of(arg_keys[2], (SLABS, M), ((0, 4),), -0.4, 0.0), -1.5, 1.5)
    onsite = gaussian(arg_keys[3], (SLABS, 2, M, M), (25 * M) ** -0.5, 0.078125, ((0, 4),), jnp.float32)
    coupling = draw_coupling(jax.random.fold_in(arg_keys[8], 71), 0)
    deform = jnp.clip(0.2 + 0.8 * jax.random.uniform(arg_keys[5], (SLABS, M, M), jnp.float32) ** steps_of(arg_keys[5], (SLABS, M, M), ((0, 4),), -0.2, 0.2), 0.2, 1.0)
    offsets = draw_offsets(jax.random.fold_in(arg_keys[8], 71), 0)
    weights = set_ends(jax.random.randint(arg_keys[7], (OFFSETS,), 8, 41), jax.random.fold_in(arg_keys[7], 1), 8, 40).astype(jnp.int32)
    return dict(energy_real=energy_real, energy_imag=energy_imag, potential=potential, onsite=onsite, coupling=coupling, deform=deform, offsets=offsets, weights=weights)


def matmul_high(left, right):
    return jnp.matmul(left, right, precision=lax.Precision.HIGHEST)


def complex_mul(left, right):
    left_real, left_imag = left[..., 0, :, :], left[..., 1, :, :]
    right_real, right_imag = right[..., 0, :, :], right[..., 1, :, :]
    real_part = matmul_high(left_real, right_real) - matmul_high(left_imag, right_imag)
    imag_part = matmul_high(left_real, right_imag) + matmul_high(left_imag, right_real)
    return jnp.stack([real_part, imag_part], axis=-3)


def adjoint(matrix):
    return jnp.stack([jnp.swapaxes(matrix[..., 0, :, :], -1, -2), -jnp.swapaxes(matrix[..., 1, :, :], -1, -2)], axis=-3)


def invert(matrix_real, matrix_imag):
    block_order = matrix_real.shape[-1]
    identity = jnp.eye(block_order, dtype=jnp.float32)
    diagonal_real = jnp.diagonal(matrix_real, axis1=-2, axis2=-1)
    diagonal_imag = jnp.diagonal(matrix_imag, axis1=-2, axis2=-1)
    modulus = diagonal_real * diagonal_real + diagonal_imag * diagonal_imag
    inverse_real = diagonal_real / modulus
    inverse_imag = -diagonal_imag / modulus
    column_real = inverse_real[..., None, :]
    column_imag = inverse_imag[..., None, :]
    product_real = matrix_real * column_real - matrix_imag * column_imag
    product_imag = matrix_real * column_imag + matrix_imag * column_real
    remainder_real = 2.0 * identity - product_real
    remainder_imag = -product_imag
    row_real = inverse_real[..., :, None]
    row_imag = inverse_imag[..., :, None]
    estimate = jnp.stack([row_real * remainder_real - row_imag * remainder_imag, row_real * remainder_imag + row_imag * remainder_real], axis=-3)
    matrix = jnp.stack([matrix_real, matrix_imag], axis=-3)
    for newton_step in range(NEWTON - 1):
        product = complex_mul(matrix, estimate)
        remainder = jnp.stack([2.0 * identity - product[..., 0, :, :], -product[..., 1, :, :]], axis=-3)
        estimate = complex_mul(estimate, remainder)
    return estimate


def reference(energy_real, energy_imag, potential, onsite, coupling, deform, offsets, weights):
    block_order = onsite.shape[-1]
    energy_count = energy_real.shape[0]
    identity = jnp.eye(block_order, dtype=jnp.float32)
    base_real = energy_real[:, None, None, None] * identity - (potential[:, :, None] * identity)[None] - onsite[None, :, 0]
    base_imag = energy_imag[:, None, None, None] * identity - onsite[None, :, 1]
    coupling_adj = adjoint(coupling)
    green = jnp.zeros((energy_count,) + onsite.shape, jnp.float32)
    sigma = jnp.zeros((energy_count,) + onsite.shape, jnp.float32)
    row_index = jnp.arange(energy_count, dtype=jnp.int32)[:, None, None]
    col_index = jnp.arange(energy_count, dtype=jnp.int32)[None, :, None]
    target = row_index + offsets[None, None, :]
    table = jnp.sum(jnp.where(col_index == target, weights.astype(jnp.float32)[None, None, :] / 128.0, jnp.float32(0.0)), axis=-1)
    for outer_step in range(OUTER):
        for sweep_step in range(SWEEPS):
            incoming = jnp.concatenate([jnp.zeros_like(green[:, :1]), green[:, :-1]], axis=1)
            couple = complex_mul(complex_mul(coupling[None], incoming), coupling_adj[None])
            green = invert(base_real - sigma[:, :, 0] - couple[:, :, 0], base_imag - sigma[:, :, 1] - couple[:, :, 1])
        summed = jnp.tensordot(table, green, axes=1, precision=lax.Precision.HIGHEST)
        sigma = deform[None, :, None] * summed
    return green, sigma
```

```python
import jax
import jax.numpy as jnp
from jax import lax
from jax.experimental import pallas as pl
from jax.experimental.pallas import tpu as pltpu
from jax.sharding import PartitionSpec as P

M = 256
ENERGIES = 128
SLABS = 4
GROUPS = 32
ROWS = 8
PAD = 8
AXES = ("energy", "slab")
F32 = jnp.float32
BF16 = jnp.bfloat16


def halves(value):
    high = value.astype(BF16)
    low = (value - high.astype(F32)).astype(BF16)
    return high, low


def left_form(real, imag):
    rh, rl = halves(real)
    ih, il = halves(imag)
    return jnp.concatenate([rh, rh, rl, ih, ih, il], axis=1)


def right_form(real, imag):
    rh, rl = halves(real)
    ih, il = halves(imag)
    to_real = jnp.concatenate([rh, rl, rh, -ih, -il, -ih], axis=0)
    to_imag = jnp.concatenate([ih, il, ih, rh, rl, rh], axis=0)
    return to_real, to_imag


def product(left, right):
    real = jnp.dot(left, right[0], preferred_element_type=F32)
    imag = jnp.dot(left, right[1], preferred_element_type=F32)
    return real, imag


def chain_kernel(own_ref, er_ref, ei_ref, h_ref, c_ref, *refs, first):
    if first:
        rest = refs
    else:
        sigma_ref, win_ref = refs[:2]
        rest = refs[2:]
    if first:
        spread_ref, wout_ref = rest[:2]
        state_ref = rest[2]
    else:
        spread_ref, natural_ref = rest[:2]
        state_ref = rest[2]
    own = own_ref[0]
    energy_real = er_ref[own]
    energy_imag = ei_ref[own]
    row = lax.broadcasted_iota(jnp.int32, (M, M), 0)
    col = lax.broadcasted_iota(jnp.int32, (M, M), 1)
    on_diagonal = row == col
    eye = jnp.where(on_diagonal, F32(1.0), F32(0.0))

    def base(slab):
        place = slab ^ own
        real = energy_real * eye - h_ref[place, 0]
        imag = energy_imag * eye - h_ref[place, 1]
        if not first:
            real = real - sigma_ref[:, slab, 0].reshape(M, M)
            imag = imag - sigma_ref[:, slab, 1].reshape(M, M)
        return real, imag

    def invert(real, imag):
        col_real = jnp.sum(jnp.where(on_diagonal, real, 0.0), axis=0, keepdims=True)
        col_imag = jnp.sum(jnp.where(on_diagonal, imag, 0.0), axis=0, keepdims=True)
        row_real = jnp.sum(jnp.where(on_diagonal, real, 0.0), axis=1, keepdims=True)
        row_imag = jnp.sum(jnp.where(on_diagonal, imag, 0.0), axis=1, keepdims=True)
        col_mod = 1.0 / (col_real * col_real + col_imag * col_imag)
        row_mod = 1.0 / (row_real * row_real + row_imag * row_imag)
        dcr, dci = col_real * col_mod, -col_imag * col_mod
        drr, dri = row_real * row_mod, -row_imag * row_mod
        rest_real = jnp.where(on_diagonal, 0.0, imag * dci - real * dcr)
        rest_imag = jnp.where(on_diagonal, 0.0, -(real * dci + imag * dcr))
        left = left_form(rest_real, rest_imag)
        sq_real, sq_imag = product(left, right_form(rest_real, rest_imag))
        cube_real, cube_imag = product(left, right_form(sq_real, sq_imag))
        sum_real = eye + rest_real + sq_real + cube_real
        sum_imag = rest_imag + sq_imag + cube_imag
        return drr * sum_real - dri * sum_imag, drr * sum_imag + dri * sum_real

    def couple(slab, real, imag):
        place = slab ^ own
        cr = c_ref[place, 0]
        ci = c_ref[place, 1]
        left_real, left_imag = product(left_form(cr, ci), right_form(real, imag))
        return product(left_form(left_real, left_imag), right_form(cr.T, -ci.T))

    def keep(slab, real, imag):
        spread_ref[:, slab, 0] = real.reshape(GROUPS, ROWS, M)
        spread_ref[:, slab, 1] = imag.reshape(GROUPS, ROWS, M)
        if not first:
            natural_ref[slab ^ own, 0] = real
            natural_ref[slab ^ own, 1] = imag

    for item in range(2):
        real, imag = base(item)
        if item == 1 and not first:
            real = real - win_ref[0]
            imag = imag - win_ref[1]
        real, imag = invert(real, imag)
        state_ref[item, 0] = real
        state_ref[item, 1] = imag
        if item == 0:
            keep(0, real, imag)

    def stage(step, carry):
        for item in range(2):
            slab = step + item
            add_real, add_imag = couple(slab, state_ref[item, 0], state_ref[item, 1])
            if first and item == 0:

                @pl.when(step == 1)
                def _():
                    wout_ref[0] = add_real
                    wout_ref[1] = add_imag

            real, imag = base(slab)
            real, imag = invert(real - add_real, imag - add_imag)
            state_ref[item, 0] = real
            state_ref[item, 1] = imag
            if item == 0:
                keep(slab, real, imag)
            else:

                @pl.when(step == 2)
                def _():
                    keep(3, real, imag)

        return carry

    lax.fori_loop(1, 3, stage, 0)


def run_chain(own, energy_real, energy_imag, blocks, coupling, sigma, carried):
    first = sigma is None
    smem = pl.BlockSpec(memory_space=pltpu.SMEM)
    vmem = pl.BlockSpec(memory_space=pltpu.VMEM)
    spread = jax.ShapeDtypeStruct((GROUPS, SLABS, 2, ROWS, M), F32)
    if first:
        second = jax.ShapeDtypeStruct((2, M, M), F32)
        operands = (own, energy_real, energy_imag, blocks, coupling)
    else:
        second = jax.ShapeDtypeStruct((SLABS, 2, M, M), F32)
        operands = (own, energy_real, energy_imag, blocks, coupling, sigma, carried)
    return pl.pallas_call(
        lambda *refs: chain_kernel(*refs, first=first),
        out_shape=(spread, second),
        in_specs=[smem] * 3 + [vmem] * (len(operands) - 3),
        out_specs=(vmem, vmem),
        scratch_shapes=[pltpu.VMEM((2, 2, M, M), F32)],
        compiler_params=pltpu.CompilerParams(vmem_limit_bytes=48 * 1024 * 1024),
        name="chain_first" if first else "chain_second",
    )(*operands)


def mix_kernel(offsets_ref, weights_ref, green_ref, deform_ref, out_ref, padded_ref):
    zeros = jnp.zeros((PAD, 2, ROWS, M), F32)
    padded_ref[:PAD] = zeros
    padded_ref[PAD + ENERGIES :] = zeros
    padded_ref[PAD : PAD + ENERGIES] = green_ref[...]
    deform = deform_ref[...]
    scale = [weights_ref[k].astype(F32) * (1.0 / 128.0) for k in range(8)]
    shift = [offsets_ref[k] + PAD for k in range(8)]

    def body(energy, carry):
        total = scale[0] * padded_ref[energy + shift[0]]
        for k in range(1, 8):
            total = total + scale[k] * padded_ref[energy + shift[k]]
        out_ref[energy] = deform[None] * total
        return carry

    lax.fori_loop(0, ENERGIES, body, 0, unroll=4)


def mix(offsets, weights, green, deform):
    smem = pl.BlockSpec(memory_space=pltpu.SMEM)
    vmem = pl.BlockSpec(memory_space=pltpu.VMEM)
    return pl.pallas_call(
        mix_kernel,
        out_shape=jax.ShapeDtypeStruct((ENERGIES, 2, ROWS, M), F32),
        in_specs=[smem, smem, vmem, vmem],
        out_specs=vmem,
        scratch_shapes=[pltpu.VMEM((ENERGIES + 2 * PAD, 2, ROWS, M), F32)],
        compiler_params=pltpu.CompilerParams(vmem_limit_bytes=32 * 1024 * 1024),
        name="mix",
    )(offsets, weights, green, deform)


def linear(group, slab):
    return group * SLABS + slab


def within_chip(flip):
    return [
        (linear(group, slab), linear(group, slab ^ flip))
        for group in range(GROUPS)
        for slab in range(SLABS)
    ]


def from_beside():
    return [(linear(group, slab), linear(group ^ 1, slab ^ 2)) for group in range(GROUPS) for slab in range(SLABS)]


def on_device(energy_real, energy_imag, potential, onsite, coupling, deform, offsets, weights):
    own = lax.axis_index("slab").astype(jnp.int32).reshape(1)
    group = lax.axis_index("energy")
    identity = jnp.eye(M, dtype=F32)
    blocks = jnp.stack(
        [onsite[0, 0] + potential[0][:, None] * identity, onsite[0, 1], coupling[0, 0], coupling[0, 1]]
    )
    across = lax.ppermute(blocks, AXES, from_beside())
    beside = lax.ppermute(blocks, AXES, within_chip(1))
    across_beside = lax.ppermute(across, AXES, within_chip(1))
    every = [blocks, beside, across, across_beside]
    block_all = jnp.stack([part[:2] for part in every])
    coupling_all = jnp.stack([part[2:] for part in every])
    deform_rows = lax.dynamic_slice(deform[0], (group * ROWS, 0), (ROWS, M))

    spread, carried = run_chain(own, energy_real, energy_imag, block_all, coupling_all, None, None)
    gathered = lax.all_to_all(spread.reshape(ENERGIES, 2, ROWS, M), AXES, 0, 0, tiled=True)
    mixed = mix(offsets, weights, gathered, deform_rows)
    sigma = lax.all_to_all(mixed, AXES, 0, 0, tiled=True)
    sigma = sigma.reshape(GROUPS, SLABS, 2, ROWS, M)

    spread, natural = run_chain(own, energy_real, energy_imag, block_all, coupling_all, sigma, carried)
    pieces = [natural[0]]
    for flip in range(1, SLABS):
        pieces.append(lax.ppermute(natural[flip], AXES, within_chip(flip)))
    gathered = lax.all_to_all(spread.reshape(ENERGIES, 2, ROWS, M), AXES, 0, 0, tiled=True)
    mixed = mix(offsets, weights, gathered, deform_rows)
    parts = mixed.reshape(GROUPS, 4, 2, ROWS, M)
    parts = lax.all_to_all(parts, "energy", 0, 0, tiled=True)
    self_energy = jnp.transpose(parts, (1, 2, 0, 3, 4)).reshape(4, 1, 2, M, M)
    green = jnp.zeros((4, 1, 2, M, M), F32)
    for flip in range(SLABS):
        green = lax.dynamic_update_slice(
            green, pieces[flip][None, None], (own[0] ^ flip, 0, 0, 0, 0)
        )
    return (green, self_energy)


def solution(mesh):
    return jax.shard_map(
        on_device,
        mesh=mesh,
        in_specs=(
            P("energy"),
            P("energy"),
            P("slab", None),
            P("slab", None, None, None),
            P("slab", None, None, None),
            P("slab", None, None),
            P(),
            P(),
        ),
        out_specs=(P("energy", "slab", None, None, None), P("energy", "slab", None, None, None)),
        check_vma=False,
    )
```

```python
import jax
import jax.numpy as jnp
from jax import lax
from jax.experimental import pallas as pl
from jax.experimental.pallas import tpu as pltpu
from jax.sharding import PartitionSpec as P

M = 256
ENERGIES = 128
OFFSETS = 8
SLABS = 4
GROUPS = 32
ROWS = 8
PAD = 8
AXES = ("energy", "slab")
F32 = jnp.float32
BF16 = jnp.bfloat16


def halves(value):
    high = value.astype(BF16)
    low = (value - high.astype(F32)).astype(BF16)
    return high, low


def triple(high, low, axis):
    return jnp.concatenate([high, low, high] if axis == 0 else [high, high, low], axis=axis)


def left_form(real, imag):
    return [triple(*halves(value), 1) for value in (real + imag, real, imag)]


def right_form(real, imag):
    return [triple(*halves(value), 0) for value in (real, imag - real, real + imag)]


def product(left, right):
    parts = [jnp.dot(left[k], right[k], preferred_element_type=F32) for k in range(3)]
    return parts[0] - parts[2], parts[0] + parts[1]


def tools():
    row = lax.broadcasted_iota(jnp.int32, (M, M), 0)
    col = lax.broadcasted_iota(jnp.int32, (M, M), 1)
    on_diagonal = row == col
    eye = jnp.where(on_diagonal, F32(1.0), F32(0.0))
    return on_diagonal, eye


def invert(real, imag, on_diagonal, eye):
    only_real = jnp.where(on_diagonal, real, 0.0)
    only_imag = jnp.where(on_diagonal, imag, 0.0)
    col_real = jnp.sum(only_real, axis=0, keepdims=True)
    col_imag = jnp.sum(only_imag, axis=0, keepdims=True)
    row_real = jnp.sum(only_real, axis=1, keepdims=True)
    row_imag = jnp.sum(only_imag, axis=1, keepdims=True)
    col_mod = 1.0 / (col_real * col_real + col_imag * col_imag)
    row_mod = 1.0 / (row_real * row_real + row_imag * row_imag)
    dcr, dci = col_real * col_mod, -col_imag * col_mod
    drr, dri = row_real * row_mod, -row_imag * row_mod
    off_real = real - only_real
    off_imag = imag - only_imag
    rest_real = off_imag * dci - off_real * dcr
    rest_imag = -(off_real * dci + off_imag * dcr)
    real_halves = halves(rest_real)
    both_halves = halves(rest_real + rest_imag)
    left = [triple(*both_halves, 1), triple(*real_halves, 1), triple(*halves(rest_imag), 1)]
    right = [triple(*real_halves, 0), triple(*halves(rest_imag - rest_real), 0), triple(*both_halves, 0)]
    sq_real, sq_imag = product(left, right)
    cube_real, cube_imag = product(left, right_form(sq_real, sq_imag))
    sum_real = eye + rest_real + sq_real + cube_real
    sum_imag = rest_imag + sq_imag + cube_imag
    return drr * sum_real - dri * sum_imag, drr * sum_imag + dri * sum_real


def fill(own, parts, target, sems):
    copies = []
    for flip in range(len(parts)):
        copies.append(pltpu.make_async_copy(parts[flip], target.at[own ^ flip], sems.at[flip]))
    for copy in copies:
        copy.start()
    return copies


def specs():
    return (
        pl.BlockSpec(memory_space=pltpu.SMEM),
        pl.BlockSpec(memory_space=pltpu.VMEM),
        pl.BlockSpec(memory_space=pl.ANY),
    )


def seed_kernel(own_ref, count_ref, er_ref, ei_ref, *refs):
    h_parts = refs[:4]
    out_ref, h_ref, sems = refs[4:]
    own = own_ref[0]
    count = count_ref[0]
    copies = fill(own, h_parts, h_ref, sems)
    on_diagonal, eye = tools()
    for copy in copies:
        copy.wait()

    def body(step, carry):
        index = jnp.where(step == count, OFFSETS, step)
        energy_real = er_ref[index]
        energy_imag = ei_ref[index]
        for slab in range(2):
            real, imag = invert(
                energy_real * eye - h_ref[slab, 0],
                energy_imag * eye - h_ref[slab, 1],
                on_diagonal,
                eye,
            )
            out_ref[index, slab, 0] = real
            out_ref[index, slab, 1] = imag
        return carry

    lax.fori_loop(0, count + 1, body, 0)


def run_seed(own, count, energy_real, energy_imag, blocks):
    smem, vmem, anywhere = specs()
    return pl.pallas_call(
        seed_kernel,
        out_shape=jax.ShapeDtypeStruct((OFFSETS + 1, 2, 2, M, M), F32),
        in_specs=[smem] * 4 + [anywhere] * 4,
        out_specs=vmem,
        scratch_shapes=[pltpu.VMEM((SLABS, 2, M, M), F32), pltpu.SemaphoreType.DMA((SLABS,))],
        compiler_params=pltpu.CompilerParams(vmem_limit_bytes=40 * 1024 * 1024),
        name="seed",
    )(own, count, energy_real, energy_imag, *blocks)


def chain_kernel(own_ref, count_ref, er_ref, ei_ref, scale_ref, *refs):
    own = own_ref[0]
    count = count_ref[0]
    h_parts, c_parts, d_parts, seed_ref = refs[:4], refs[4:8], refs[8:12], refs[12]
    spread_ref, natural_ref = refs[13:15]
    h_ref, c_ref, d_ref, left_ref, right_ref, state_ref, sum_ref, sems, seed_sems = refs[15:]
    copies = fill(own, c_parts, c_ref, sems.at[1])
    late_copies = fill(own, h_parts, h_ref, sems.at[0]) + fill(own, d_parts, d_ref, sems.at[2])

    def seed_copy(step):
        index = jnp.where(step == count, OFFSETS, step)
        slot = step % 2
        return pltpu.make_async_copy(seed_ref.at[index], state_ref.at[slot], seed_sems.at[slot])

    seed_copy(0).start()
    on_diagonal, eye = tools()
    sum_ref[...] = jnp.zeros_like(sum_ref)
    for copy in copies:
        copy.wait()
    for slab in range(1, SLABS):
        cr = c_ref[slab, 0]
        ci = c_ref[slab, 1]
        left = left_form(cr, ci)
        right = right_form(cr.T, -ci.T)
        for k in range(3):
            left_ref[slab - 1, k] = left[k]
            right_ref[slab - 1, k] = right[k]
    for copy in late_copies:
        copy.wait()

    def couple(slab, real, imag):
        left = [left_ref[slab - 1, k] for k in range(3)]
        right = [right_ref[slab - 1, k] for k in range(3)]
        mid_real, mid_imag = product(left, right_form(real, imag))
        return product(left_form(mid_real, mid_imag), right)

    def stages(base, start):
        state = start
        finals = [start[0]]
        for step in (1, 2):
            results = []
            for item in range(2):
                slab = step + item
                add_real, add_imag = couple(slab, *state[item])
                real, imag = base(slab)
                results.append(invert(real - add_real, imag - add_imag, on_diagonal, eye))
            state = results
            finals.append(state[0])
        finals.append(state[1])
        return finals

    def body(step, carry):
        slot = step % 2
        seed_copy(step).wait()
        seed_copy(step + 1).start()
        energy_real = er_ref[step]
        energy_imag = ei_ref[step]
        scale = scale_ref[step]

        def base(slab):
            return energy_real * eye - h_ref[slab, 0], energy_imag * eye - h_ref[slab, 1]

        start = [(state_ref[slot, item, 0], state_ref[slot, item, 1]) for item in range(2)]
        finals = stages(base, start)
        for slab in range(SLABS):
            for part in range(2):
                sum_ref[slab, part] += scale * finals[slab][part]
        return carry

    lax.fori_loop(0, count, body, 0)
    seed_copy(count).wait()
    slot = count % 2
    energy_real = er_ref[OFFSETS]
    energy_imag = ei_ref[OFFSETS]

    def base(slab):
        deform = d_ref[slab]
        real = energy_real * eye - h_ref[slab, 0] - deform * sum_ref[slab, 0]
        imag = energy_imag * eye - h_ref[slab, 1] - deform * sum_ref[slab, 1]
        return real, imag

    add_real, add_imag = couple(1, state_ref[slot, 0, 0], state_ref[slot, 0, 1])
    real, imag = base(1)
    start = [
        invert(*base(0), on_diagonal, eye),
        invert(real - add_real, imag - add_imag, on_diagonal, eye),
    ]
    finals = stages(base, start)
    for slab in range(SLABS):
        for part in range(2):
            value = finals[slab][part]
            spread_ref[:, slab, part] = value.reshape(GROUPS, ROWS, M)
            natural_ref[own ^ slab, part] = value


def run_chain(own, count, energy_real, energy_imag, scale, blocks, couplings, deforms, seeds):
    smem, vmem, anywhere = specs()
    return pl.pallas_call(
        chain_kernel,
        out_shape=(
            jax.ShapeDtypeStruct((GROUPS, SLABS, 2, ROWS, M), F32),
            jax.ShapeDtypeStruct((SLABS, 2, M, M), F32),
        ),
        in_specs=[smem] * 5 + [anywhere] * 13,
        out_specs=(vmem, vmem),
        scratch_shapes=[
            pltpu.VMEM((SLABS, 2, M, M), F32),
            pltpu.VMEM((SLABS, 2, M, M), F32),
            pltpu.VMEM((SLABS, M, M), F32),
            pltpu.VMEM((SLABS - 1, 3, M, 3 * M), BF16),
            pltpu.VMEM((SLABS - 1, 3, 3 * M, M), BF16),
            pltpu.VMEM((2, 2, 2, M, M), F32),
            pltpu.VMEM((SLABS, 2, M, M), F32),
            pltpu.SemaphoreType.DMA((3, SLABS)),
            pltpu.SemaphoreType.DMA((2,)),
        ],
        compiler_params=pltpu.CompilerParams(vmem_limit_bytes=52 * 1024 * 1024),
        name="chain",
    )(own, count, energy_real, energy_imag, scale, *blocks, *couplings, *deforms, seeds)


def mix_kernel(offsets_ref, weights_ref, green_ref, deform_ref, out_ref, padded_ref):
    deform = deform_ref[...]
    inner = green_ref.shape[1:]
    zeros = jnp.zeros((PAD,) + inner, F32)
    padded_ref[:PAD] = zeros
    padded_ref[PAD + ENERGIES :] = zeros
    padded_ref[PAD : PAD + ENERGIES] = green_ref[...]
    scale = [weights_ref[k].astype(F32) * (1.0 / 128.0) for k in range(8)]
    shift = [offsets_ref[k] + PAD for k in range(8)]

    def body(energy, carry):
        total = scale[0] * padded_ref[energy + shift[0]]
        for k in range(1, 8):
            total = total + scale[k] * padded_ref[energy + shift[k]]
        out_ref[energy] = deform[None] * total
        return carry

    lax.fori_loop(0, ENERGIES, body, 0, unroll=4)


def mix(offsets, weights, green, deform):
    smem, vmem, anywhere = specs()
    return pl.pallas_call(
        mix_kernel,
        out_shape=jax.ShapeDtypeStruct(green.shape, F32),
        in_specs=[smem, smem, vmem, vmem],
        out_specs=vmem,
        scratch_shapes=[pltpu.VMEM((ENERGIES + 2 * PAD,) + green.shape[1:], F32)],
        compiler_params=pltpu.CompilerParams(vmem_limit_bytes=32 * 1024 * 1024),
        name="mix",
    )(offsets, weights, green, deform)


def linear(group, slab):
    return group * SLABS + slab


def within_chip(flip):
    return [
        (linear(group, slab), linear(group, slab ^ flip))
        for group in range(GROUPS)
        for slab in range(SLABS)
    ]


def from_beside():
    return [(linear(group, slab), linear(group ^ 1, slab ^ 2)) for group in range(GROUPS) for slab in range(SLABS)]


def spread_params(value):
    across = lax.ppermute(value, AXES, from_beside())
    beside = lax.ppermute(value, AXES, within_chip(1))
    across_beside = lax.ppermute(across, AXES, within_chip(1))
    return [value, beside, across, across_beside]


def from_group(value, by):
    pairs = [(i, i + by) for i in range(GROUPS) if 0 <= i + by < GROUPS]
    return lax.ppermute(value, "energy", pairs)


def on_device(energy_real, energy_imag, potential, onsite, coupling, deform, offsets, weights):
    slab = lax.axis_index("slab").astype(jnp.int32)
    own = slab.reshape(1)
    group = lax.axis_index("energy")
    identity = jnp.eye(M, dtype=F32)
    block = jnp.stack([onsite[0, 0] + potential[0][:, None] * identity, onsite[0, 1]])
    blocks = spread_params(block)
    couplings = spread_params(coupling[0])
    deforms = spread_params(deform[0])
    energy = jnp.stack([energy_real, energy_imag])
    window = jnp.concatenate([from_group(energy, 2), from_group(energy, 1), energy, from_group(energy, -1), from_group(energy, -2)], axis=1)
    target = 4 * group + slab + offsets
    inside = (target >= 0) & (target < ENERGIES)
    order = jnp.arange(OFFSETS, dtype=jnp.int32)
    same = offsets[:, None] == offsets[None, :]
    earlier = order[None, :] < order[:, None]
    used = inside & ~jnp.any(same & earlier, axis=1)
    merged = jnp.sum(jnp.where(same, weights[None, :], 0), axis=1)
    slot = jnp.sum(jnp.where(earlier & used[None, :], 1, 0), axis=1)
    count = jnp.sum(used.astype(jnp.int32)).reshape(1)
    chosen = used[None, :] & (slot[None, :] == order[:, None])
    scale = jnp.sum(jnp.where(chosen, merged[None, :], 0), axis=1).astype(F32) * (1.0 / 128.0)
    place = jnp.sum(jnp.where(chosen, offsets[None, :], 0), axis=1) + 8 + slab
    place = jnp.concatenate([place, jnp.reshape(8 + slab, (1,))])
    hot = place[:, None] == jnp.arange(20, dtype=jnp.int32)[None]
    near_real = jnp.sum(jnp.where(hot, window[0][None], 0.0), axis=1)
    near_imag = jnp.sum(jnp.where(hot, window[1][None], 0.0), axis=1)
    deform_rows = lax.dynamic_slice(deform[0], (group * ROWS, 0), (ROWS, M))

    seeds = run_seed(own, count, near_real, near_imag, blocks)
    spread, natural = run_chain(
        own, count, near_real, near_imag, scale, blocks, couplings, deforms, seeds
    )
    pieces = [natural[0]]
    for flip in range(1, SLABS):
        pieces.append(lax.ppermute(natural[flip], AXES, within_chip(flip)))
    gathered = lax.all_to_all(spread.reshape(ENERGIES, 2, ROWS, M), AXES, 0, 0, tiled=True)
    mixed = mix(offsets, weights, gathered, deform_rows)
    parts = mixed.reshape(GROUPS, 4, 2, ROWS, M)
    parts = lax.all_to_all(parts, "energy", 0, 0, tiled=True)
    self_energy = jnp.transpose(parts, (1, 2, 0, 3, 4)).reshape(4, 1, 2, M, M)
    green = jnp.zeros((4, 1, 2, M, M), F32)
    for flip in range(SLABS):
        green = lax.dynamic_update_slice(green, pieces[flip][None, None], (slab ^ flip, 0, 0, 0, 0))
    return (green, self_energy)


def solution(mesh):
    return jax.shard_map(
        on_device,
        mesh=mesh,
        in_specs=(
            P("energy"),
            P("energy"),
            P("slab", None),
            P("slab", None, None, None),
            P("slab", None, None, None),
            P("slab", None, None),
            P(),
            P(),
        ),
        out_specs=(P("energy", "slab", None, None, None), P("energy", "slab", None, None, None)),
        check_vma=False,
    )
```
